32 devices in a mesh: groups: 2 (over x), date: 16 (over z, y, core).
Axes of the slice: x: 2, y: 2, z: 4, core: 2. Of those that a mesh axis runs over, the one named last changes fastest.
Arguments:
- images: float32 [32, 2, 64, 2560], P(('groups', 'date')), parts along dimension 0, may hold values from -16 to 16
- height_phase: float32 [128, 2560], P(('groups', 'date')), parts along dimension 0, may hold values from -4 to 4
- baseline: float32 [32], P('groups'), parts along dimension 0, may hold values from -0.6 to 0.6
- pair_list: int32 [32, 2], replicated, may hold values from 0 to 15, as said below
- pair_owner: int32 [32, 1], replicated, may hold values from 0 to 15; in each aligned block of 32 rows (0 to 31, 32 to 63, ...) at most 4 rows name the same one
Outputs:
- interferogram: float32 [128, 2, 16, 128], P(('groups', 'date')), parts along dimension 0
- coherence: float32 [128, 16, 128], P(('groups', 'date')), parts along dimension 0
The draws below stay inside these ranges and needn't reach their ends.
There are 2 independent parts, one for each index of `groups`. The reference program is written for one: setup_inputs(seed, part) draws one part's arguments, and reference() takes and returns one part's arrays. A program takes and returns all parts, laid end to end along the dimension named above; an argument that names none is the same for every part. Nothing has to cross between parts.
Inputs may be any that keep to these rules, and one draw needn't show every extreme that they name: `pair_list`: each row is (r, s) with r < s <= r + 4; some pair has s = r + 4. `pair_owner`: every index owns at least one pair and at most 4 pairs; some index owns exactly 4.
All inputs are finite; a program needn't handle non-finite values.
Results may differ from the reference program's by a relative error of at most 0.00007.
Values sent between devices are 32-bit elements; how exact they have to be, the bound alone decides.
A program may use at most 128 MiB of HBM per device.

```python
import math
import jax
import jax.numpy as jnp
import numpy as np
from jax import lax

LOOK_ROWS = 4
LOOK_COLS = 20
BAND = 4
CAP = 4
COLS = 2560
DATES = 16
PAIRS = 32
ROWS = 64
N_DATE = 16


def draw_images(key, part):
    common = jax.random.normal(jax.random.fold_in(key, 101), (2, ROWS, COLS), jnp.float32)
    noise = jax.random.normal(jax.random.fold_in(key, 102), (DATES, 2, ROWS, COLS), jnp.float32)
    spread = math.log(10.0) / 4.0
    low_rho = 0.3
    high_rho = 0.95
    row_scale = jnp.exp(jax.random.uniform(jax.random.fold_in(key, 105), (ROWS,), jnp.float32, -spread, spread))
    col_scale = jnp.exp(jax.random.uniform(jax.random.fold_in(key, 106), (COLS,), jnp.float32, -spread, spread))
    amplitude = row_scale[:, None] * col_scale[None, :]
    rho_value = jax.random.uniform(jax.random.fold_in(key, 107), (DATES,), jnp.float32, low_rho, high_rho)
    angle_value = jax.random.uniform(jax.random.fold_in(key, 108), (DATES,), jnp.float32, -math.pi, math.pi)
    cosine = jnp.cos(angle_value)[:, None, None]
    sine_part = jnp.sin(angle_value)[:, None, None]
    common_real = cosine * common[0][None] - sine_part * common[1][None]
    common_imag = sine_part * common[0][None] + cosine * common[1][None]
    rest = jnp.sqrt(1.0 - rho_value * rho_value)[:, None, None]
    rho_wide = rho_value[:, None, None]
    real_part = amplitude[None] * (rho_wide * common_real + rest * noise[:, 0])
    imag_part = amplitude[None] * (rho_wide * common_imag + rest * noise[:, 1])
    return jnp.clip(jnp.stack([real_part, imag_part], axis=1), -16.0, 16.0).astype(jnp.float32)


def draw_pair_list(key, part):
    first_date = jax.random.randint(jax.random.fold_in(key, 201), (PAIRS,), 0, DATES - BAND, jnp.int32)
    distance = jax.random.randint(jax.random.fold_in(key, 202), (PAIRS,), 1, BAND + 1, jnp.int32)
    position = jnp.arange(PAIRS, dtype=jnp.int32)
    distance = jnp.where(position == 0, BAND, distance)
    return jnp.stack([first_date, first_date + distance], axis=1).astype(jnp.int32)


def shard_levels(own_key, extent, cuts, smallest, largest):
    factor_of = 1.0
    for axis_at, parts in cuts:
        draws = jax.random.uniform(jax.random.fold_in(jax.random.fold_in(own_key, 6), axis_at), (parts,), jnp.float32, smallest / len(cuts), largest / len(cuts))
        factor_of = factor_of * jnp.repeat(jnp.exp(draws), extent[axis_at] // parts).reshape((-1,) + (1,) * (len(extent) - 1 - axis_at))
    return factor_of


def shared_out(own_key, own, number, rows, amount, top, limit, slope):
    sequence = jax.random.permutation(own_key, amount)
    crowded, ordinary = shares(amount, rows * top, limit, slope, True), shares(amount, rows * top, limit, slope, False)
    places = jnp.arange(amount)

    def named(lengths, rotation):
        used = int((lengths > 0).sum())
        fixed = max(1, used // 4)
        passed = fixed + (places - fixed + rotation * (used - fixed)) % max(1, amount - fixed)
        return jnp.zeros((amount,), jnp.int32).at[sequence[jnp.where(places < fixed, places, passed)]].set(jnp.asarray(lengths, jnp.int32))

    lengths = jnp.where(number % 4 == 0, named(crowded, number // 4), named(ordinary, number - number // 4 - 1))
    mixed = jax.random.permutation(jax.random.fold_in(own, 3), amount)
    giver, sink = mixed[0:amount // 2 * 2:2], mixed[1:amount // 2 * 2:2]
    slack = jnp.minimum(lengths[giver] - 1, limit - lengths[sink]) // 2
    slack = jnp.where((giver == sequence[0]) | (sink == sequence[0]) | (lengths[sink] == 0), 0, jnp.maximum(slack, 0))
    passed = jax.random.randint(jax.random.fold_in(own, 4), (amount // 2,), 0, 1 << 20) % (slack + 1)
    lengths = lengths.at[giver].add(-passed).at[sink].add(passed)
    labels = jnp.searchsorted(jnp.cumsum(lengths), jnp.arange(rows * top), side="right").astype(jnp.int32)
    grid = labels.reshape(top, rows).T
    grid = grid[jax.random.permutation(jax.random.fold_in(own, 1), rows)]
    rotation = jax.random.randint(jax.random.fold_in(own, 2), (rows, 1), 0, top)
    return jnp.take_along_axis(grid, (jnp.arange(top)[None, :] + rotation) % top, axis=1)


def shares(number_of, total, bound, skew, full):
    weights = [(1 << 20) // math.isqrt(standing ** skew) + 1 for standing in range(1, number_of + 1)]
    largest = bound if full else min(bound, max(-(-total // number_of), total * weights[0] // sum(weights)))
    least = 1 if total - largest >= number_of - 1 else 0
    counts, spare = [largest] + [least] * (number_of - 1), total - largest - least * (number_of - 1)
    while spare > 0:
        free = [i for i in range(1, number_of) if counts[i] < largest] or [i for i in range(1, number_of) if counts[i] < bound]
        mass, remaining = sum([weights[i] for i in free]), spare
        for i in free:
            extra = min(bound - counts[i], max(1, remaining * weights[i] // mass), spare)
            counts[i] = counts[i] + extra
            spare = spare - extra
    return np.array(counts)


def scatter_about(rng, extent, scale, limit, pieces=(), held_as=jnp.bfloat16):
    values = scale * jax.random.normal(rng, extent, jnp.float32)
    if pieces:
        values = values * shard_levels(rng, extent, pieces, -0.22, 0.18)
    return jnp.clip(values, -limit, limit).astype(held_as)


def setup_inputs(seed: int = 0, part: int = 0) -> dict:
    splits = jax.random.split(jax.random.key(seed), 6)
    part_splits = jax.random.split(jax.random.fold_in(splits[5], part), 6)
    images = draw_images(jax.random.fold_in(jax.random.fold_in(splits[5], part), 71), part)
    height_phase = scatter_about(part_splits[1], (ROWS, COLS), 1.0, 4.0, ((0, 16),), jnp.float32)
    baseline = jnp.clip(jax.random.uniform(part_splits[2], (DATES,), jnp.float32, -0.6, 0.6), -0.6, 0.6)
    pair_list = draw_pair_list(jax.random.fold_in(splits[5], 71), part)
    pair_owner_keys = jax.random.split(jax.random.fold_in(splits[4], 1), PAIRS // PAIRS)
    pair_owner_turns = jax.random.permutation(jax.random.fold_in(splits[4], 3), PAIRS // PAIRS)
    pair_owner = jax.vmap(lambda own, number: shared_out(jax.random.fold_in(splits[4], 2), own, number, PAIRS, N_DATE, 1, CAP, 2))(pair_owner_keys, pair_owner_turns).reshape((PAIRS, 1))
    return {"images": images, "height_phase": height_phase, "baseline": baseline, "pair_list": pair_list, "pair_owner": pair_owner}


EPSILON = 1e-06

def multilook(values):
    values_shape = values.shape
    grouped = values.reshape(values_shape[:-2] + (values_shape[-2] // LOOK_ROWS, LOOK_ROWS, values_shape[-1] // LOOK_COLS, LOOK_COLS))
    return lax.optimization_barrier(jnp.mean(grouped, axis=(-3, -1)))

def flatten_phase(images, factors, height_phase):
    phase_angle = factors[:, None, None] * height_phase[None]
    cosine = jnp.cos(phase_angle)
    sine_part = jnp.sin(phase_angle)
    real_part = images[:, 0] * cosine - images[:, 1] * sine_part
    imag_part = images[:, 0] * sine_part + images[:, 1] * cosine
    return (real_part, imag_part)

def slot_of(pair_owner):
    owners = pair_owner[:, 0]
    position = jnp.arange(owners.shape[0], dtype=jnp.int32)
    earlier = (owners[:, None] == owners[None, :]) & (position[:, None] > position[None, :])
    return (owners * CAP + lax.optimization_barrier(jnp.sum(earlier.astype(jnp.int32), axis=1))).astype(jnp.int32)

def reference(images, height_phase, baseline, pair_list, pair_owner):
    real_part, imag_part = flatten_phase(images, baseline, height_phase)
    power_map = multilook(real_part * real_part + imag_part * imag_part)

    def one_pair(pair_row):
        first_date = pair_row[0]
        second_date = pair_row[1]
        first_real = real_part[first_date]
        first_imag = imag_part[first_date]
        second_real = real_part[second_date]
        second_imag = imag_part[second_date]
        look_real = multilook(first_real * second_real + first_imag * second_imag)
        look_imag = multilook(first_imag * second_real - first_real * second_imag)
        denominator = jnp.sqrt((power_map[first_date] + EPSILON) * (power_map[second_date] + EPSILON))
        coherence = jnp.sqrt(look_real * look_real + look_imag * look_imag) / denominator
        return jnp.stack([look_real, look_imag, coherence])
    results = lax.map(one_pair, pair_list)
    slot_index = slot_of(pair_owner)
    filled = jnp.zeros((CAP * N_DATE,) + results.shape[1:], jnp.float32).at[slot_index].set(results)
    return (filled[:, :2], filled[:, 2])
```

```python
import functools

import jax
import jax.numpy as jnp
from jax import lax
from jax.experimental import pallas as pl
from jax.experimental.pallas import tpu as pltpu
from jax.sharding import PartitionSpec as P

LOOK_ROWS = 4
LOOK_COLS = 20
CAP = 4
BAND = 4
EPSILON = 1e-06
LANES = 128
TILE = 8
GROUP = 16


def split(values, parts):
    pieces = []
    for _ in range(parts):
        piece = values.astype(jnp.bfloat16)
        pieces.append(piece)
        values = values - piece.astype(jnp.float32)
    return pieces


def kernel(
    devices, chunks, images, height, baseline, pair_list, pair_owner, looks_out, coherence_out,
    recv, heights, cosines, sines, box, sums, pick_look, pick_first, pick_second,
    stack_real, stack_imag, stack_power, outbox, inbox,
    send_sem, recv_sem, own_sem, height_sem, out_send_sem, out_recv_sem,
):
    me = lax.axis_index("date")
    half = images.shape[2] // 2
    width = half // chunks
    core = lax.rem(me, 2)
    partner = me + 1 - 2 * core

    def peer(step):
        return lax.rem(me + step, devices)

    barrier = pltpu.get_barrier_semaphore()

    @pl.loop(1, devices)
    def _(step):
        pl.semaphore_signal(barrier, inc=1, device_id={"date": peer(step)})

    pl.semaphore_wait(barrier, devices - 1)

    def lines(target, chunk):
        first = pl.multiple_of(lax.div(target, 2) * TILE, TILE)
        column = pl.multiple_of(lax.rem(target, 2) * half + chunk * width, LANES)
        return images.at[:, pl.ds(first, TILE), pl.ds(column, width)]

    def landing(source, chunk):
        return recv.at[chunk, :, pl.ds(pl.multiple_of(source * TILE, TILE), TILE), :]

    def line_copy(target, chunk):
        return pltpu.make_async_remote_copy(
            src_ref=lines(target, chunk),
            dst_ref=landing(me, chunk),
            send_sem=send_sem.at[chunk, target],
            recv_sem=recv_sem.at[chunk, me],
            device_id={"date": target},
        )

    def line_arrival(source, chunk):
        return pltpu.make_async_remote_copy(
            src_ref=lines(source, chunk),
            dst_ref=landing(source, chunk),
            send_sem=send_sem.at[chunk, source],
            recv_sem=recv_sem.at[chunk, source],
            device_id={"date": source},
        )

    def own_copy(chunk):
        return pltpu.make_async_copy(lines(me, chunk), landing(me, chunk), own_sem.at[chunk])

    def columns_of(which):
        return height.at[:, pl.ds(pl.multiple_of(which * half, LANES), half)]

    height_own = pltpu.make_async_copy(columns_of(core), heights.at[core], height_sem.at[0])
    height_away = pltpu.make_async_remote_copy(
        src_ref=columns_of(1 - core),
        dst_ref=heights.at[core],
        send_sem=height_sem.at[1],
        recv_sem=height_sem.at[2],
        device_id={"date": partner},
    )
    height_own.start()
    height_away.start()

    @pl.loop(0, chunks)
    def _(chunk):
        @pl.loop(1, devices)
        def _(step):
            line_copy(peer(step), chunk).start()

        own_copy(chunk).start()

    rows = box.shape[0]
    position = lax.broadcasted_iota(jnp.int32, (rows, LANES), 0)
    target = lax.broadcasted_iota(jnp.int32, (rows, LANES), 1) * LOOK_COLS
    box[...] = jnp.where(
        (position >= target) & (position < target + LOOK_COLS), 1.0, 0.0
    ).astype(jnp.bfloat16)

    def as_column(row):
        size = row.shape[1]
        down = lax.broadcasted_iota(jnp.int32, (size, size), 0)
        across = lax.broadcasted_iota(jnp.int32, (size, size), 1)
        return jnp.sum(
            jnp.where(down == across, jnp.broadcast_to(row, (size, size)), 0.0), axis=1, keepdims=True
        )

    owner = pair_owner[...].astype(jnp.float32)
    pairs = owner.shape[1]
    down = lax.broadcasted_iota(jnp.int32, (pairs, pairs), 0)
    across = lax.broadcasted_iota(jnp.int32, (pairs, pairs), 1)
    earlier = (as_column(owner) == owner) & (down < across)
    place = owner * GROUP + jnp.sum(jnp.where(earlier, 1.0, 0.0), axis=0, keepdims=True)
    first = pair_list[0:1, :].astype(jnp.float32)
    second = pair_list[1:2, :].astype(jnp.float32)
    band = (second - first - 1.0) * devices + first
    total = devices * GROUP
    line = lax.broadcasted_iota(jnp.int32, (total, pairs), 0)
    line = (line - (line & 12)).astype(jnp.float32)
    taken = line == place

    def listed(value):
        return jnp.sum(jnp.where(taken, value + 1.0, 0.0), axis=1, keepdims=True) - 1.0

    def one_hot(value, size):
        lane = lax.broadcasted_iota(jnp.int32, (total, 3 * size), 1) & (size - 1)
        return jnp.where(lane.astype(jnp.float32) == value, 1.0, 0.0).astype(jnp.bfloat16)

    pick_look[...] = one_hot(listed(band), BAND * devices)
    pick_first[...] = one_hot(listed(first), devices)
    pick_second[...] = one_hot(listed(second), devices)
    scale = as_column(baseline[...])
    sums[...] = jnp.zeros_like(sums)

    height_own.wait()
    height_away.wait()

    for row in range(TILE):
        @pl.loop(0, half // LANES)
        def _(block):
            column = pl.ds(pl.multiple_of(block * LANES, LANES), LANES)
            level = heights[row // LOOK_ROWS, row % LOOK_ROWS:row % LOOK_ROWS + 1, column]
            angle = scale * level
            cosines[row, :, column] = jnp.cos(angle)
            sines[row, :, column] = jnp.sin(angle)

    @pl.loop(0, chunks)
    def _(chunk):
        own_copy(chunk).wait()

        @pl.loop(1, devices)
        def _(step):
            line_arrival(peer(step), chunk).wait_recv()

        column = pl.multiple_of(chunk * width, width)
        outer = pl.ds(column, width)
        summed = sums[...]
        for look_row in range(TILE // LOOK_ROWS):
            totals = [None] * (1 + 2 * BAND)

            def add(at, value):
                totals[at] = value if totals[at] is None else totals[at] + value

            for row in range(look_row * LOOK_ROWS, (look_row + 1) * LOOK_ROWS):
                real = recv[chunk, 0, pl.ds(row, devices, stride=TILE), :]
                imag = recv[chunk, 1, pl.ds(row, devices, stride=TILE), :]
                cosine = cosines[row, :, outer]
                sine = sines[row, :, outer]
                flat_real = real * cosine - imag * sine
                flat_imag = real * sine + imag * cosine
                add(0, flat_real * flat_real + flat_imag * flat_imag)
                for distance in range(1, BAND + 1):
                    next_real = pltpu.roll(flat_real, devices - distance, 0)
                    next_imag = pltpu.roll(flat_imag, devices - distance, 0)
                    add(distance, flat_real * next_real + flat_imag * next_imag)
                    add(BAND + distance, flat_imag * next_real - flat_real * next_imag)
            weights = box[pl.ds(pl.multiple_of(look_row * half + column, width), width), :]
            pieces = split(jnp.concatenate(totals, axis=0), 2)
            for piece in pieces:
                summed = summed + jnp.dot(piece, weights, preferred_element_type=jnp.float32)
        sums[...] = summed

    mean = sums[...] * (1.0 / (LOOK_ROWS * LOOK_COLS))
    ends = (0, devices, (1 + BAND) * devices, (1 + 2 * BAND) * devices)
    for stack, low, high in zip((stack_power, stack_real, stack_imag), ends[:-1], ends[1:]):
        for part, piece in enumerate(split(mean[low:high], 3)):
            stack[part * (high - low):(part + 1) * (high - low), :] = piece

    def chosen(pick, stack):
        return jnp.dot(pick[...], stack[...], preferred_element_type=jnp.float32)

    look_real = chosen(pick_look, stack_real)
    look_imag = chosen(pick_look, stack_imag)
    denominator = jnp.sqrt(
        (chosen(pick_first, stack_power) + EPSILON) * (chosen(pick_second, stack_power) + EPSILON)
    )
    ratio = jnp.sqrt(look_real * look_real + look_imag * look_imag) / denominator
    kind = lax.broadcasted_iota(jnp.int32, (total, LANES), 0) & 12
    outbox[...] = jnp.where(kind == 0, look_real, jnp.where(kind == 4, look_imag, ratio))

    def parcel(which):
        return pl.ds(pl.multiple_of(which * GROUP, GROUP), GROUP)

    def out_copy(target):
        return pltpu.make_async_remote_copy(
            src_ref=outbox.at[parcel(target), :],
            dst_ref=inbox.at[parcel(me), :],
            send_sem=out_send_sem.at[target],
            recv_sem=out_recv_sem.at[me],
            device_id={"date": target},
        )

    def out_arrival(source):
        return pltpu.make_async_remote_copy(
            src_ref=outbox.at[parcel(source), :],
            dst_ref=inbox.at[parcel(source), :],
            send_sem=out_send_sem.at[source],
            recv_sem=out_recv_sem.at[source],
            device_id={"date": source},
        )

    @pl.loop(1, devices)
    def _(step):
        out_copy(peer(step)).start()

    inbox[parcel(me), :] = outbox[parcel(me), :]

    @pl.loop(0, chunks)
    def _(chunk):
        @pl.loop(1, devices)
        def _(step):
            line_copy(peer(step), chunk).wait_send()

    @pl.loop(1, devices)
    def _(step):
        out_arrival(peer(step)).wait_recv()

    left = lax.broadcasted_iota(jnp.int32, (devices // 2, LANES), 1) < LANES // 2
    for kind_at in range(3):
        for slot in range(CAP):
            at = kind_at * CAP + slot
            even = inbox[pl.ds(at, devices // 2, stride=2 * GROUP), :]
            odd = inbox[pl.ds(GROUP + at, devices // 2, stride=2 * GROUP), :]
            upper = jnp.where(left, even, pltpu.roll(odd, LANES // 2, 1))
            lower = jnp.where(left, pltpu.roll(even, LANES // 2, 1), odd)
            for look_row, value in enumerate((upper, lower)):
                lines_at = pl.ds(look_row, devices // 2, stride=2)
                if kind_at < 2:
                    looks_out[slot, kind_at, lines_at, :] = value
                else:
                    coherence_out[slot, lines_at, :] = value

    @pl.loop(1, devices)
    def _(step):
        out_copy(peer(step)).wait_send()


def body(images, height_phase, baseline, pair_list, pair_owner):
    devices = lax.axis_size("date")
    rows, columns = images.shape[2:]
    half = columns // 2
    width = LANES
    chunks = half // width
    lanes = columns // LOOK_COLS
    assert lanes == LANES and rows == LOOK_ROWS * devices and half % LANES == 0
    quantities = 1 + 2 * BAND
    total = devices * GROUP
    vmem = pl.BlockSpec(memory_space=pltpu.VMEM)
    anywhere = pl.BlockSpec(memory_space=pl.ANY)
    return pl.pallas_call(
        functools.partial(kernel, devices, chunks),
        out_shape=(
            jax.ShapeDtypeStruct((CAP, 2, devices, lanes), jnp.float32),
            jax.ShapeDtypeStruct((CAP, devices, lanes), jnp.float32),
        ),
        in_specs=[anywhere, anywhere, vmem, vmem, vmem],
        out_specs=(vmem, vmem),
        scratch_shapes=[
            pltpu.VMEM((chunks, 2, devices * TILE, width), jnp.float32),
            pltpu.VMEM((2, LOOK_ROWS, half), jnp.float32),
            pltpu.VMEM((TILE, devices, half), jnp.float32),
            pltpu.VMEM((TILE, devices, half), jnp.float32),
            pltpu.VMEM((columns, lanes), jnp.bfloat16),
            pltpu.VMEM((quantities * devices, lanes), jnp.float32),
            pltpu.VMEM((total, 3 * BAND * devices), jnp.bfloat16),
            pltpu.VMEM((total, 3 * devices), jnp.bfloat16),
            pltpu.VMEM((total, 3 * devices), jnp.bfloat16),
            pltpu.VMEM((3 * BAND * devices, lanes), jnp.bfloat16),
            pltpu.VMEM((3 * BAND * devices, lanes), jnp.bfloat16),
            pltpu.VMEM((3 * devices, lanes), jnp.bfloat16),
            pltpu.VMEM((total, lanes), jnp.float32),
            pltpu.VMEM((total, lanes), jnp.float32),
            pltpu.SemaphoreType.DMA((chunks, devices)),
            pltpu.SemaphoreType.DMA((chunks, devices)),
            pltpu.SemaphoreType.DMA((chunks,)),
            pltpu.SemaphoreType.DMA((3,)),
            pltpu.SemaphoreType.DMA((devices,)),
            pltpu.SemaphoreType.DMA((devices,)),
        ],
        compiler_params=pltpu.CompilerParams(collective_id=0, has_side_effects=True),
    )(images[0], height_phase, baseline[None], pair_list.T, pair_owner.T)


def solution(mesh):
    in_specs = (
        P(("groups", "date"), None, None, None),
        P(("groups", "date"), None),
        P("groups"),
        P(),
        P(),
    )
    out_specs = (P(("groups", "date"), None, None, None), P(("groups", "date"), None, None))
    return jax.shard_map(body, mesh=mesh, in_specs=in_specs, out_specs=out_specs, check_vma=False)
```

```python
import functools
import math

import jax
import jax.numpy as jnp
from jax import lax
from jax.experimental import pallas as pl
from jax.experimental.pallas import tpu as pltpu
from jax.sharding import PartitionSpec as P

LOOK_ROWS = 4
LOOK_COLS = 20
CAP = 4
BAND = 4
EPSILON = 1e-06
LANES = 128
TILE = 8
LAG = 3


def split(values, parts):
    pieces = []
    for _ in range(parts):
        piece = values.astype(jnp.bfloat16)
        pieces.append(piece)
        values = values - piece.astype(jnp.float32)
    return pieces


def cos_sin(angle):
    square = angle * angle
    sine = jnp.full_like(angle, -1.0 / math.factorial(15))
    for term in range(6, -1, -1):
        sine = sine * square + (-1.0) ** term / math.factorial(2 * term + 1)
    cosine = jnp.full_like(angle, 1.0 / math.factorial(16))
    for term in range(7, -1, -1):
        cosine = cosine * square + (-1.0) ** term / math.factorial(2 * term)
    return cosine, sine * angle


def kernel(
    devices, images, height, baseline, pair_list, pair_owner, looks_out, coherence_out,
    window, heights, box, sums, pick_look, pick_first, pick_second,
    stack_real, stack_imag, stack_power, outbox, inbox,
    plane_send, relay_send, plane_recv, relay_recv, height_send, height_recv, out_send, out_recv,
):
    me = lax.axis_index("date")
    planes = devices // BAND
    plane = lax.div(me, BAND)
    spot = lax.rem(me, BAND)
    rows, columns = images.shape[1:]
    blocks = columns // LANES
    tiles = rows // (2 * BAND * TILE)
    chunks = tiles * blocks
    side = BAND * TILE
    sources = devices // BAND
    look_rows = TILE // LOOK_ROWS

    def peer(step):
        return lax.rem(me + step, devices)

    barrier = pltpu.get_barrier_semaphore()

    @pl.loop(1, devices)
    def _(step):
        pl.semaphore_signal(barrier, inc=1, device_id={"date": peer(step)})

    pl.semaphore_wait(barrier, devices - 1)

    def lines(quarter, upper, chunk):
        first = ((quarter * 2 + upper) * tiles + lax.div(chunk, blocks)) * TILE
        column = lax.rem(chunk, blocks) * LANES
        return images.at[
            :, pl.ds(pl.multiple_of(first, TILE), TILE), pl.ds(pl.multiple_of(column, LANES), LANES)
        ]

    def place(upper, chunk, slot, size=TILE):
        return window.at[upper, chunk, :, pl.ds(pl.multiple_of(slot * TILE, TILE), size), :]

    def own_slot(upper, which):
        return (1 - upper) * BAND + which

    def plane_copy(step, upper, chunk):
        to = spot ^ step
        return pltpu.make_async_remote_copy(
            src_ref=lines(to, upper, chunk),
            dst_ref=place(upper, chunk, own_slot(upper, spot)),
            send_sem=plane_send.at[upper, chunk],
            recv_sem=plane_recv.at[upper, chunk, spot],
            device_id={"date": plane * BAND + to},
        )

    def plane_arrival(step, upper, chunk):
        source = spot ^ step
        return pltpu.make_async_remote_copy(
            src_ref=lines(source, upper, chunk),
            dst_ref=place(upper, chunk, own_slot(upper, source)),
            send_sem=plane_send.at[upper, chunk],
            recv_sem=plane_recv.at[upper, chunk, source],
            device_id={"date": plane * BAND + source},
        )

    def own_copy(upper, chunk):
        return pltpu.make_async_copy(
            lines(spot, upper, chunk),
            place(upper, chunk, own_slot(upper, spot)),
            plane_recv.at[upper, chunk, spot],
        )

    def relays(upper):
        return plane < planes - 1 if upper == 0 else plane > 0

    def gets_relays(upper):
        return plane > 0 if upper == 0 else plane < planes - 1

    def relay_copy(upper, chunk, which, source):
        return pltpu.make_async_remote_copy(
            src_ref=source,
            dst_ref=place(upper, chunk, upper * BAND + which),
            send_sem=relay_send.at[upper, chunk],
            recv_sem=relay_recv.at[upper, chunk],
            device_id={"date": me + BAND * (1 - 2 * upper)},
        )

    def relay_all(upper, chunk):
        return pltpu.make_async_remote_copy(
            src_ref=place(upper, chunk, (1 - upper) * BAND, side),
            dst_ref=place(upper, chunk, upper * BAND, side),
            send_sem=relay_send.at[upper, chunk],
            recv_sem=relay_recv.at[upper, chunk],
            device_id={"date": me},
        )

    def plane_all(upper, chunk):
        return pltpu.make_async_remote_copy(
            src_ref=place(upper, chunk, 0, side - TILE),
            dst_ref=place(upper, chunk, 0, side - TILE),
            send_sem=plane_send.at[upper, chunk],
            recv_sem=relay_recv.at[upper, chunk],
            device_id={"date": me},
        )

    reader = lax.div(me, sources)
    own_height = lax.rem(me, sources)

    def height_copy(to_plane):
        return pltpu.make_async_remote_copy(
            src_ref=height,
            dst_ref=heights.at[own_height],
            send_sem=height_send.at[to_plane],
            recv_sem=height_recv.at[own_height],
            device_id={"date": to_plane * BAND + reader},
        )

    def height_own():
        return pltpu.make_async_copy(height, heights.at[own_height], height_recv.at[own_height])

    def height_arrival(source):
        return pltpu.make_async_remote_copy(
            src_ref=height,
            dst_ref=heights.at[source],
            send_sem=height_send.at[0],
            recv_sem=height_recv.at[source],
            device_id={"date": me},
        )

    @pl.loop(0, planes)
    def _(to_plane):
        @pl.when(to_plane * BAND + reader != me)
        def _():
            height_copy(to_plane).start()

        @pl.when(to_plane * BAND + reader == me)
        def _():
            height_own().start()

    @pl.loop(0, chunks)
    def _(chunk):
        for upper in range(2):
            for step in (2, 3, 1):
                plane_copy(step, upper, chunk).start()

            @pl.when(relays(upper))
            def _():
                relay_copy(upper, chunk, spot, lines(spot, upper, chunk)).start()

            own_copy(upper, chunk).start()

    for upper in range(2):
        @pl.when(jnp.logical_not(gets_relays(upper)))
        def _():
            @pl.loop(0, chunks)
            def _(chunk):
                window[upper, chunk, :, upper * side:(upper + 1) * side, :] = jnp.zeros(
                    (2, side, LANES), jnp.float32
                )

    position = lax.broadcasted_iota(jnp.int32, (columns, LANES), 0)
    target = lax.broadcasted_iota(jnp.int32, (columns, LANES), 1) * LOOK_COLS
    box[...] = jnp.where(
        (position >= target) & (position < target + LOOK_COLS), 1.0, 0.0
    ).astype(jnp.bfloat16)
    sums[...] = jnp.zeros_like(sums)

    dates = 2 * BAND
    lane = lax.broadcasted_iota(jnp.int32, (dates, devices), 1)
    date = lax.broadcasted_iota(jnp.int32, (dates, devices), 0)
    scales = []
    for upper in range(2):
        chosen_date = lane == date + (plane - 1 + upper) * BAND
        scales.append(
            jnp.sum(jnp.where(chosen_date, baseline[...], 0.0), axis=1, keepdims=True)
        )

    owner = pair_owner[...].astype(jnp.float32)
    pairs = owner.shape[1]
    down = lax.broadcasted_iota(jnp.int32, (pairs, pairs), 0)
    across = lax.broadcasted_iota(jnp.int32, (pairs, pairs), 1)
    owner_column = jnp.sum(jnp.where(down == across, owner, 0.0), axis=1, keepdims=True)
    earlier = (owner_column == owner) & (down < across)
    spot_of = owner * TILE + jnp.sum(jnp.where(earlier, 1.0, 0.0), axis=0, keepdims=True)
    first = pair_list[0:1, :]
    second = pair_list[1:2, :]
    total = devices * TILE
    line = lax.broadcasted_iota(jnp.int32, (total, pairs), 0)
    taken = (line - (line & CAP)).astype(jnp.float32) == spot_of

    def pick(value, valid, size):
        lane = lax.broadcasted_iota(jnp.int32, (total, 3 * size), 1) & (size - 1)
        listed = jnp.sum(
            jnp.where(taken & valid, value.astype(jnp.float32) + 1.0, 0.0), axis=1, keepdims=True
        ) - 1.0
        return jnp.where(lane.astype(jnp.float32) == listed, 1.0, 0.0).astype(jnp.bfloat16)

    for upper in range(2):
        ends_here = second if upper == 0 else first
        valid = (ends_here >= plane * BAND) & (ends_here < (plane + 1) * BAND)
        start = first - (plane - 1 + upper) * BAND
        distance = second - first
        pick_look[upper] = pick((distance - 1) * dates + start, valid, BAND * dates)
        pick_first[upper] = pick(start, valid, dates)
        pick_second[upper] = pick(start + distance, valid, dates)

    @pl.loop(0, sources)
    def _(source):
        height_arrival(source).wait_recv()

    def forward(chunk):
        for upper in range(2):
            own_copy(upper, chunk).wait()
        for step in (1, 2, 3):
            for upper in range(2):
                plane_arrival(step, upper, chunk).wait_recv()

                @pl.when(relays(upper))
                def _():
                    which = spot ^ step
                    relay_copy(
                        upper, chunk, which, place(upper, chunk, own_slot(upper, which))
                    ).start()

    def compute(chunk):
        for upper in range(2):
            @pl.when(gets_relays(upper))
            def _():
                relay_all(upper, chunk).wait_recv()

        tile = lax.div(chunk, blocks)
        column = pl.multiple_of(lax.rem(chunk, blocks) * LANES, LANES)
        totals = []
        for upper in range(2):
            for look_row in range(look_rows):
                found = [None] * (1 + 2 * BAND)

                def add(at, value):
                    found[at] = value if found[at] is None else found[at] + value

                source = (upper * tiles + tile) * look_rows + look_row
                for row in range(LOOK_ROWS):
                    level = heights[source, row:row + 1, pl.ds(column, LANES)]
                    cosine, sine = cos_sin(scales[upper] * level)
                    at = pl.ds(look_row * LOOK_ROWS + row, dates, stride=TILE)
                    real = window[upper, chunk, 0, at, :]
                    imag = window[upper, chunk, 1, at, :]
                    flat_real = real * cosine - imag * sine
                    flat_imag = real * sine + imag * cosine
                    add(0, flat_real * flat_real + flat_imag * flat_imag)
                    for distance in range(1, BAND + 1):
                        next_real = pltpu.roll(flat_real, dates - distance, 0)
                        next_imag = pltpu.roll(flat_imag, dates - distance, 0)
                        add(distance, flat_real * next_real + flat_imag * next_imag)
                        add(BAND + distance, flat_imag * next_real - flat_real * next_imag)
                totals.extend(found)
        weights = box[pl.ds(column, LANES), :]
        summed = sums[tile]
        for piece in split(jnp.concatenate(totals, axis=0), 2):
            summed = summed + jnp.dot(piece, weights, preferred_element_type=jnp.float32)
        sums[tile] = summed

    @pl.loop(0, LAG)
    def _(chunk):
        forward(chunk)

    @pl.loop(LAG, chunks)
    def _(chunk):
        forward(chunk)
        compute(chunk - LAG)

    @pl.loop(chunks - LAG, chunks)
    def _(chunk):
        compute(chunk)

    def chosen(pick_matrix, stack):
        return jnp.dot(pick_matrix, stack[...], preferred_element_type=jnp.float32)

    kind = lax.broadcasted_iota(jnp.int32, (total, LANES), 0) & CAP
    quantities = (1 + 2 * BAND) * dates
    ends = (0, dates, (1 + BAND) * dates, quantities)
    for tile in range(tiles):
        mean = sums[tile] * (1.0 / (LOOK_ROWS * LOOK_COLS))
        for upper in range(2):
            ratios = []
            for look_row in range(look_rows):
                base = (upper * look_rows + look_row) * quantities
                for stack, low, high in zip((stack_power, stack_real, stack_imag), ends[:-1], ends[1:]):
                    size = high - low
                    stack[...] = jnp.concatenate(
                        [p.astype(jnp.float32) for p in split(mean[base + low:base + high], 3)], axis=0
                    ).astype(jnp.bfloat16)
                look_real = chosen(pick_look[upper], stack_real)
                look_imag = chosen(pick_look[upper], stack_imag)
                denominator = jnp.sqrt(
                    (chosen(pick_first[upper], stack_power) + EPSILON)
                    * (chosen(pick_second[upper], stack_power) + EPSILON)
                )
                ratios.append(jnp.sqrt(look_real * look_real + look_imag * look_imag) / denominator)
                outbox[(tile * 2 + upper) * 3 + look_row] = jnp.where(kind == 0, look_real, look_imag)
            outbox[(tile * 2 + upper) * 3 + 2] = jnp.where(kind == 0, ratios[0], ratios[1])

    def parcel(which):
        return pl.ds(pl.multiple_of(which * TILE, TILE), TILE)

    def out_copy(to):
        return pltpu.make_async_remote_copy(
            src_ref=outbox.at[:, parcel(to), :],
            dst_ref=inbox.at[me],
            send_sem=out_send.at[to],
            recv_sem=out_recv.at[me],
            device_id={"date": to},
        )

    def out_arrival(source):
        return pltpu.make_async_remote_copy(
            src_ref=outbox.at[:, parcel(source), :],
            dst_ref=inbox.at[source],
            send_sem=out_send.at[source],
            recv_sem=out_recv.at[source],
            device_id={"date": source},
        )

    @pl.loop(1, devices)
    def _(step):
        out_copy(peer(step)).start()

    inbox[me] = outbox[:, parcel(me), :]

    @pl.loop(0, planes)
    def _(to_plane):
        @pl.when(to_plane * BAND + reader != me)
        def _():
            height_copy(to_plane).wait_send()

    @pl.loop(0, chunks)
    def _(chunk):
        for upper in range(2):
            plane_all(upper, chunk).wait_send()

            @pl.when(relays(upper))
            def _():
                relay_all(upper, chunk).wait_send()

    @pl.loop(1, devices)
    def _(step):
        out_arrival(peer(step)).wait_recv()

    height_rows = 2 * tiles * look_rows * BAND
    for quarter in range(BAND):
        for tile in range(tiles):
            for upper in range(2):
                for part in range(3):
                    value = inbox[quarter, (tile * 2 + upper) * 3 + part]
                    for other in range(1, planes):
                        value = value + inbox[other * BAND + quarter, (tile * 2 + upper) * 3 + part]
                    row = ((quarter * 2 + upper) * tiles + tile) * look_rows
                    for c in range(2):
                        piece = value[c * CAP:(c + 1) * CAP]
                        if part < 2:
                            looks_out[pl.ds(c * height_rows + row + part, CAP, stride=2 * height_rows), :] = piece
                        else:
                            coherence_out[pl.ds(row + c, CAP, stride=height_rows), :] = piece

    @pl.loop(1, devices)
    def _(step):
        out_copy(peer(step)).wait_send()


def body(images, height_phase, baseline, pair_list, pair_owner):
    devices = lax.axis_size("date")
    rows, columns = images.shape[2:]
    lanes = columns // LOOK_COLS
    looks = rows // LOOK_ROWS
    tiles = rows // (2 * BAND * TILE)
    chunks = tiles * (columns // LANES)
    dates = 2 * BAND
    assert lanes == LANES and rows == LOOK_ROWS * devices and TILE == 2 * LOOK_ROWS
    assert rows % (2 * BAND * TILE) == 0 and columns % LANES == 0
    quantities = 1 + 2 * BAND
    total = devices * TILE
    vmem = pl.BlockSpec(memory_space=pltpu.VMEM)
    hbm = pl.BlockSpec(memory_space=pltpu.HBM)
    look, coherence = pl.pallas_call(
        functools.partial(kernel, devices),
        out_shape=(
            jax.ShapeDtypeStruct((CAP * 2 * looks, lanes), jnp.float32),
            jax.ShapeDtypeStruct((CAP * looks, lanes), jnp.float32),
        ),
        in_specs=[hbm, hbm, vmem, vmem, vmem],
        out_specs=(vmem, vmem),
        scratch_shapes=[
            pltpu.VMEM((2, chunks, 2, dates * TILE, LANES), jnp.float32),
            pltpu.VMEM((devices // BAND, LOOK_ROWS, columns), jnp.float32),
            pltpu.VMEM((columns, lanes), jnp.bfloat16),
            pltpu.VMEM((tiles, 4 * quantities * dates, lanes), jnp.float32),
            pltpu.VMEM((2, total, 3 * BAND * dates), jnp.bfloat16),
            pltpu.VMEM((2, total, 3 * dates), jnp.bfloat16),
            pltpu.VMEM((2, total, 3 * dates), jnp.bfloat16),
            pltpu.VMEM((3 * BAND * dates, lanes), jnp.bfloat16),
            pltpu.VMEM((3 * BAND * dates, lanes), jnp.bfloat16),
            pltpu.VMEM((3 * dates, lanes), jnp.bfloat16),
            pltpu.VMEM((tiles * 6, total, lanes), jnp.float32),
            pltpu.VMEM((devices, tiles * 6, TILE, lanes), jnp.float32),
            pltpu.SemaphoreType.DMA((2, chunks)),
            pltpu.SemaphoreType.DMA((2, chunks)),
            pltpu.SemaphoreType.DMA((2, chunks, BAND)),
            pltpu.SemaphoreType.DMA((2, chunks)),
            pltpu.SemaphoreType.DMA((devices // BAND,)),
            pltpu.SemaphoreType.DMA((devices // BAND,)),
            pltpu.SemaphoreType.DMA((devices,)),
            pltpu.SemaphoreType.DMA((devices,)),
        ],
        compiler_params=pltpu.CompilerParams(
            collective_id=0, has_side_effects=True, vmem_limit_bytes=44 << 20
        ),
    )(images[0], height_phase, baseline[None], pair_list.T, pair_owner.T)
    return look.reshape(CAP, 2, looks, lanes), coherence.reshape(CAP, looks, lanes)


def solution(mesh):
    in_specs = (
        P(("groups", "date"), None, None, None),
        P(("groups", "date"), None),
        P("groups"),
        P(),
        P(),
    )
    out_specs = (P(("groups", "date"), None, None, None), P(("groups", "date"), None, None))
    return jax.shard_map(body, mesh=mesh, in_specs=in_specs, out_specs=out_specs, check_vma=False)
```

```python
import functools
import math

import jax
import jax.numpy as jnp
from jax import lax
from jax.experimental import pallas as pl
from jax.experimental.pallas import tpu as pltpu
from jax.sharding import PartitionSpec as P

LOOK_ROWS = 4
LOOK_COLS = 20
CAP = 4
BAND = 4
EPSILON = 1e-06
LANES = 128
TILE = 8
LAG = 5
AHEAD = 8


def split(values, parts):
    pieces = []
    for _ in range(parts):
        piece = values.astype(jnp.bfloat16)
        pieces.append(piece)
        values = values - piece.astype(jnp.float32)
    return pieces


def cos_sin(angle):
    square = angle * angle
    sine = jnp.full_like(angle, -1.0 / math.factorial(15))
    for term in range(6, -1, -1):
        sine = sine * square + (-1.0) ** term / math.factorial(2 * term + 1)
    cosine = jnp.full_like(angle, 1.0 / math.factorial(16))
    for term in range(7, -1, -1):
        cosine = cosine * square + (-1.0) ** term / math.factorial(2 * term)
    return cosine, sine * angle


def kernel(
    devices, images, height, baseline, pair_list, pair_owner, looks_out, coherence_out,
    window, heights, box, sums, pick_look, pick_first, pick_second,
    stack_real, stack_imag, stack_power, outbox, inbox,
    plane_send, relay_send, plane_recv, relay_recv, height_send, height_recv, out_send, out_recv,
):
    me = lax.axis_index("date")
    planes = devices // BAND
    plane = lax.div(me, BAND)
    spot = lax.rem(me, BAND)
    rows, columns = images.shape[1:]
    blocks = columns // LANES
    tiles = rows // (2 * BAND * TILE)
    chunks = tiles * blocks
    side = BAND * TILE
    sources = devices // BAND
    look_rows = TILE // LOOK_ROWS

    def peer(step):
        return lax.rem(me + step, devices)

    barrier = pltpu.get_barrier_semaphore()

    @pl.loop(1, devices)
    def _(step):
        pl.semaphore_signal(barrier, inc=1, device_id={"date": peer(step)})

    pl.semaphore_wait(barrier, devices - 1)

    def lines(quarter, upper, chunk):
        first = ((quarter * 2 + upper) * tiles + lax.div(chunk, blocks)) * TILE
        column = lax.rem(chunk, blocks) * LANES
        return images.at[
            :, pl.ds(pl.multiple_of(first, TILE), TILE), pl.ds(pl.multiple_of(column, LANES), LANES)
        ]

    def place(upper, chunk, slot, size=TILE):
        return window.at[upper, chunk, :, pl.ds(pl.multiple_of(slot * TILE, TILE), size), :]

    def own_slot(upper, which):
        return (1 - upper) * BAND + which

    def plane_copy(step, upper, chunk):
        to = spot ^ step
        return pltpu.make_async_remote_copy(
            src_ref=lines(to, upper, chunk),
            dst_ref=place(upper, chunk, own_slot(upper, spot)),
            send_sem=plane_send.at[upper, chunk],
            recv_sem=plane_recv.at[upper, chunk, spot],
            device_id={"date": plane * BAND + to},
        )

    def plane_arrival(step, upper, chunk):
        source = spot ^ step
        return pltpu.make_async_remote_copy(
            src_ref=lines(source, upper, chunk),
            dst_ref=place(upper, chunk, own_slot(upper, source)),
            send_sem=plane_send.at[upper, chunk],
            recv_sem=plane_recv.at[upper, chunk, source],
            device_id={"date": plane * BAND + source},
        )

    def own_copy(upper, chunk):
        return pltpu.make_async_copy(
            lines(spot, upper, chunk),
            place(upper, chunk, own_slot(upper, spot)),
            plane_recv.at[upper, chunk, spot],
        )

    def relays(upper):
        return plane < planes - 1 if upper == 0 else plane > 0

    def gets_relays(upper):
        return plane > 0 if upper == 0 else plane < planes - 1

    def relay_copy(upper, chunk, which, source):
        return pltpu.make_async_remote_copy(
            src_ref=source,
            dst_ref=place(upper, chunk, upper * BAND + which),
            send_sem=relay_send.at[upper, chunk],
            recv_sem=relay_recv.at[upper, chunk],
            device_id={"date": me + BAND * (1 - 2 * upper)},
        )

    def relay_all(upper, chunk):
        return pltpu.make_async_remote_copy(
            src_ref=place(upper, chunk, (1 - upper) * BAND, side),
            dst_ref=place(upper, chunk, upper * BAND, side),
            send_sem=relay_send.at[upper, chunk],
            recv_sem=relay_recv.at[upper, chunk],
            device_id={"date": me},
        )

    def plane_all(upper, chunk):
        return pltpu.make_async_remote_copy(
            src_ref=place(upper, chunk, 0, side - TILE),
            dst_ref=place(upper, chunk, 0, side - TILE),
            send_sem=plane_send.at[upper, chunk],
            recv_sem=relay_recv.at[upper, chunk],
            device_id={"date": me},
        )

    reader = lax.div(me, sources)
    own_height = lax.rem(me, sources)

    def height_copy(to_plane):
        return pltpu.make_async_remote_copy(
            src_ref=height,
            dst_ref=heights.at[own_height],
            send_sem=height_send.at[to_plane],
            recv_sem=height_recv.at[own_height],
            device_id={"date": to_plane * BAND + reader},
        )

    def height_own():
        return pltpu.make_async_copy(height, heights.at[own_height], height_recv.at[own_height])

    def height_arrival(source):
        return pltpu.make_async_remote_copy(
            src_ref=height,
            dst_ref=heights.at[source],
            send_sem=height_send.at[0],
            recv_sem=height_recv.at[source],
            device_id={"date": me},
        )

    @pl.loop(0, planes)
    def _(to_plane):
        @pl.when(to_plane * BAND + reader != me)
        def _():
            height_copy(to_plane).start()

        @pl.when(to_plane * BAND + reader == me)
        def _():
            height_own().start()

    @pl.loop(0, chunks)
    def _(chunk):
        for upper in range(2):
            for step in (2, 3, 1):
                plane_copy(step, upper, chunk).start()

            @pl.when(relays(upper))
            def _():
                relay_copy(upper, chunk, spot, lines(spot, upper, chunk)).start()

            own_copy(upper, chunk).start()

    for upper in range(2):
        @pl.when(jnp.logical_not(gets_relays(upper)))
        def _():
            @pl.loop(0, chunks)
            def _(chunk):
                window[upper, chunk, :, upper * side:(upper + 1) * side, :] = jnp.zeros(
                    (2, side, LANES), jnp.float32
                )

    position = lax.broadcasted_iota(jnp.int32, (columns, LANES), 0)
    target = lax.broadcasted_iota(jnp.int32, (columns, LANES), 1) * LOOK_COLS
    box[...] = jnp.where(
        (position >= target) & (position < target + LOOK_COLS), 1.0, 0.0
    ).astype(jnp.bfloat16)
    sums[...] = jnp.zeros_like(sums)

    dates = 2 * BAND
    lane = lax.broadcasted_iota(jnp.int32, (dates, devices), 1)
    date = lax.broadcasted_iota(jnp.int32, (dates, devices), 0)
    scales = []
    for upper in range(2):
        chosen_date = lane == date + (plane - 1 + upper) * BAND
        scales.append(
            jnp.sum(jnp.where(chosen_date, baseline[...], 0.0), axis=1, keepdims=True)
        )

    owner = pair_owner[...].astype(jnp.float32)
    pairs = owner.shape[1]
    down = lax.broadcasted_iota(jnp.int32, (pairs, pairs), 0)
    across = lax.broadcasted_iota(jnp.int32, (pairs, pairs), 1)
    owner_column = jnp.sum(jnp.where(down == across, owner, 0.0), axis=1, keepdims=True)
    earlier = (owner_column == owner) & (down < across)
    spot_of = owner * TILE + jnp.sum(jnp.where(earlier, 1.0, 0.0), axis=0, keepdims=True)
    first = pair_list[0:1, :]
    second = pair_list[1:2, :]
    total = devices * TILE
    line = lax.broadcasted_iota(jnp.int32, (total, pairs), 0)
    taken = (line - (line & CAP)).astype(jnp.float32) == spot_of

    def pick(value, valid, size):
        lane = lax.broadcasted_iota(jnp.int32, (total, 3 * size), 1) & (size - 1)
        listed = jnp.sum(
            jnp.where(taken & valid, value.astype(jnp.float32) + 1.0, 0.0), axis=1, keepdims=True
        ) - 1.0
        return jnp.where(lane.astype(jnp.float32) == listed, 1.0, 0.0).astype(jnp.bfloat16)

    for upper in range(2):
        ends_here = second if upper == 0 else first
        valid = (ends_here >= plane * BAND) & (ends_here < (plane + 1) * BAND)
        start = first - (plane - 1 + upper) * BAND
        distance = second - first
        pick_look[upper] = pick((distance - 1) * dates + start, valid, BAND * dates)
        pick_first[upper] = pick(start, valid, dates)
        pick_second[upper] = pick(start + distance, valid, dates)

    def forward(chunk):
        for upper in range(2):
            own_copy(upper, chunk).wait()
        for step in (1, 2, 3):
            for upper in range(2):
                plane_arrival(step, upper, chunk).wait_recv()

                @pl.when(relays(upper))
                def _():
                    which = spot ^ step
                    relay_copy(
                        upper, chunk, which, place(upper, chunk, own_slot(upper, which))
                    ).start()

    def compute(chunk):
        for upper in range(2):
            @pl.when(gets_relays(upper))
            def _():
                relay_all(upper, chunk).wait_recv()

        tile = lax.div(chunk, blocks)
        column = pl.multiple_of(lax.rem(chunk, blocks) * LANES, LANES)
        totals = []
        for upper in range(2):
            for look_row in range(look_rows):
                found = [None] * (1 + 2 * BAND)

                def add(at, value):
                    found[at] = value if found[at] is None else found[at] + value

                source = (upper * tiles + tile) * look_rows + look_row
                for row in range(LOOK_ROWS):
                    level = heights[source, row:row + 1, pl.ds(column, LANES)]
                    cosine, sine = cos_sin(scales[upper] * level)
                    at = pl.ds(look_row * LOOK_ROWS + row, dates, stride=TILE)
                    real = window[upper, chunk, 0, at, :]
                    imag = window[upper, chunk, 1, at, :]
                    flat_real = real * cosine - imag * sine
                    flat_imag = real * sine + imag * cosine
                    add(0, flat_real * flat_real + flat_imag * flat_imag)
                    for distance in range(1, BAND + 1):
                        next_real = pltpu.roll(flat_real, dates - distance, 0)
                        next_imag = pltpu.roll(flat_imag, dates - distance, 0)
                        add(distance, flat_real * next_real + flat_imag * next_imag)
                        add(BAND + distance, flat_imag * next_real - flat_real * next_imag)
                totals.extend(found)
        weights = box[pl.ds(column, LANES), :]
        summed = sums[tile]
        for piece in split(jnp.concatenate(totals, axis=0), 2):
            summed = summed + jnp.dot(piece, weights, preferred_element_type=jnp.float32)
        sums[tile] = summed

    @pl.loop(0, AHEAD)
    def _(chunk):
        forward(chunk)

    @pl.loop(0, sources)
    def _(source):
        height_arrival(source).wait_recv()

    @pl.loop(0, AHEAD - LAG)
    def _(chunk):
        compute(chunk)

    @pl.loop(AHEAD, chunks)
    def _(chunk):
        forward(chunk)
        compute(chunk - LAG)

    @pl.loop(chunks - LAG, chunks)
    def _(chunk):
        compute(chunk)

    def chosen(pick_matrix, stack):
        return jnp.dot(pick_matrix, stack[...], preferred_element_type=jnp.float32)

    kind = lax.broadcasted_iota(jnp.int32, (total, LANES), 0) & CAP
    quantities = (1 + 2 * BAND) * dates
    ends = (0, dates, (1 + BAND) * dates, quantities)
    for tile in range(tiles):
        mean = sums[tile] * (1.0 / (LOOK_ROWS * LOOK_COLS))
        for upper in range(2):
            ratios = []
            for look_row in range(look_rows):
                base = (upper * look_rows + look_row) * quantities
                for stack, low, high in zip((stack_power, stack_real, stack_imag), ends[:-1], ends[1:]):
                    size = high - low
                    stack[...] = jnp.concatenate(
                        [p.astype(jnp.float32) for p in split(mean[base + low:base + high], 3)], axis=0
                    ).astype(jnp.bfloat16)
                look_real = chosen(pick_look[upper], stack_real)
                look_imag = chosen(pick_look[upper], stack_imag)
                denominator = jnp.sqrt(
                    (chosen(pick_first[upper], stack_power) + EPSILON)
                    * (chosen(pick_second[upper], stack_power) + EPSILON)
                )
                ratios.append(jnp.sqrt(look_real * look_real + look_imag * look_imag) / denominator)
                outbox[(tile * 2 + upper) * 3 + look_row] = jnp.where(kind == 0, look_real, look_imag)
            outbox[(tile * 2 + upper) * 3 + 2] = jnp.where(kind == 0, ratios[0], ratios[1])

    def parcel(which):
        return pl.ds(pl.multiple_of(which * TILE, TILE), TILE)

    def out_copy(to):
        return pltpu.make_async_remote_copy(
            src_ref=outbox.at[:, parcel(to), :],
            dst_ref=inbox.at[me],
            send_sem=out_send.at[to],
            recv_sem=out_recv.at[me],
            device_id={"date": to},
        )

    def out_arrival(source):
        return pltpu.make_async_remote_copy(
            src_ref=outbox.at[:, parcel(source), :],
            dst_ref=inbox.at[source],
            send_sem=out_send.at[source],
            recv_sem=out_recv.at[source],
            device_id={"date": source},
        )

    @pl.loop(1, devices)
    def _(step):
        out_copy(peer(step)).start()

    inbox[me] = outbox[:, parcel(me), :]

    @pl.loop(0, planes)
    def _(to_plane):
        @pl.when(to_plane * BAND + reader != me)
        def _():
            height_copy(to_plane).wait_send()

    @pl.loop(0, chunks)
    def _(chunk):
        for upper in range(2):
            plane_all(upper, chunk).wait_send()

            @pl.when(relays(upper))
            def _():
                relay_all(upper, chunk).wait_send()

    @pl.loop(1, devices)
    def _(step):
        out_arrival(peer(step)).wait_recv()

    height_rows = 2 * tiles * look_rows * BAND
    for quarter in range(BAND):
        for tile in range(tiles):
            for upper in range(2):
                for part in range(3):
                    value = inbox[quarter, (tile * 2 + upper) * 3 + part]
                    for other in range(1, planes):
                        value = value + inbox[other * BAND + quarter, (tile * 2 + upper) * 3 + part]
                    row = ((quarter * 2 + upper) * tiles + tile) * look_rows
                    for c in range(2):
                        piece = value[c * CAP:(c + 1) * CAP]
                        if part < 2:
                            looks_out[pl.ds(c * height_rows + row + part, CAP, stride=2 * height_rows), :] = piece
                        else:
                            coherence_out[pl.ds(row + c, CAP, stride=height_rows), :] = piece

    @pl.loop(1, devices)
    def _(step):
        out_copy(peer(step)).wait_send()


def body(images, height_phase, baseline, pair_list, pair_owner):
    devices = lax.axis_size("date")
    rows, columns = images.shape[2:]
    lanes = columns // LOOK_COLS
    looks = rows // LOOK_ROWS
    tiles = rows // (2 * BAND * TILE)
    chunks = tiles * (columns // LANES)
    dates = 2 * BAND
    assert lanes == LANES and rows == LOOK_ROWS * devices and TILE == 2 * LOOK_ROWS
    assert rows % (2 * BAND * TILE) == 0 and columns % LANES == 0
    quantities = 1 + 2 * BAND
    total = devices * TILE
    vmem = pl.BlockSpec(memory_space=pltpu.VMEM)
    hbm = pl.BlockSpec(memory_space=pltpu.HBM)
    look, coherence = pl.pallas_call(
        functools.partial(kernel, devices),
        out_shape=(
            jax.ShapeDtypeStruct((CAP * 2 * looks, lanes), jnp.float32),
            jax.ShapeDtypeStruct((CAP * looks, lanes), jnp.float32),
        ),
        in_specs=[hbm, hbm, vmem, vmem, vmem],
        out_specs=(vmem, vmem),
        scratch_shapes=[
            pltpu.VMEM((2, chunks, 2, dates * TILE, LANES), jnp.float32),
            pltpu.VMEM((devices // BAND, LOOK_ROWS, columns), jnp.float32),
            pltpu.VMEM((columns, lanes), jnp.bfloat16),
            pltpu.VMEM((tiles, 4 * quantities * dates, lanes), jnp.float32),
            pltpu.VMEM((2, total, 3 * BAND * dates), jnp.bfloat16),
            pltpu.VMEM((2, total, 3 * dates), jnp.bfloat16),
            pltpu.VMEM((2, total, 3 * dates), jnp.bfloat16),
            pltpu.VMEM((3 * BAND * dates, lanes), jnp.bfloat16),
            pltpu.VMEM((3 * BAND * dates, lanes), jnp.bfloat16),
            pltpu.VMEM((3 * dates, lanes), jnp.bfloat16),
            pltpu.VMEM((tiles * 6, total, lanes), jnp.float32),
            pltpu.VMEM((devices, tiles * 6, TILE, lanes), jnp.float32),
            pltpu.SemaphoreType.DMA((2, chunks)),
            pltpu.SemaphoreType.DMA((2, chunks)),
            pltpu.SemaphoreType.DMA((2, chunks, BAND)),
            pltpu.SemaphoreType.DMA((2, chunks)),
            pltpu.SemaphoreType.DMA((devices // BAND,)),
            pltpu.SemaphoreType.DMA((devices // BAND,)),
            pltpu.SemaphoreType.DMA((devices,)),
            pltpu.SemaphoreType.DMA((devices,)),
        ],
        compiler_params=pltpu.CompilerParams(
            collective_id=0, has_side_effects=True
        ),
    )(images[0], height_phase, baseline[None], pair_list.T, pair_owner.T)
    return look.reshape(CAP, 2, looks, lanes), coherence.reshape(CAP, looks, lanes)


def solution(mesh):
    in_specs = (
        P(("groups", "date"), None, None, None),
        P(("groups", "date"), None),
        P("groups"),
        P(),
        P(),
    )
    out_specs = (P(("groups", "date"), None, None, None), P(("groups", "date"), None, None))
    return jax.shard_map(body, mesh=mesh, in_specs=in_specs, out_specs=out_specs, check_vma=False)
```
